32 devices in a mesh: row: 8 (over z, x), col: 4 (over y, core).
Axes of the slice: x: 2, y: 2, z: 4, core: 2. Of those that a mesh axis runs over, the one named last changes fastest.
Arguments:
- matrix: float32 [32768, 2048], P('row', 'col'), may hold values from -6 to 6
- leaf_vectors: float32 [3, 32768, 128], P(None, ('row', 'col')), may hold values from -0.09375 to 0.09375
- leaf_factors: float32 [3, 1024, 128], P(None, ('row', 'col')), may hold values from -1.5 to 1.5
- tree_vectors: float32 [3, 1024, 128], P(None, ('row', 'col')), may hold values from -0.5 to 0.5
- tree_factors: float32 [3, 1024, 128], P(None, ('row', 'col')), may hold values from -0.875 to 0.875
Outputs:
- updated: float32 [32768, 2048], P('row', 'col')
The draws below stay inside these ranges and needn't reach their ends.
All inputs are finite; a program needn't handle non-finite values.
Results may differ from the reference program's by a relative error of at most 0.0001.
Values sent between devices are 32-bit elements; how exact they have to be, the bound alone decides.
A program may use at most 128 MiB of HBM per device.

```python
import jax
import jax.numpy as jnp
from jax import lax

B = 128
M_DEV = 4096
TICKS = 3
NROWS = 32768
NCOLS = 2048
LEVELS = 3
N_ROW = 8


def levels(own_key, extent, pieces, least, high):
    gain, own = 1.0, jax.random.fold_in(own_key, 6)
    for dim, blocks in pieces:
        draws = jnp.exp(jax.random.uniform(jax.random.fold_in(own, dim), (blocks,), jnp.float32, least / len(pieces), high / len(pieces)))
        gain = gain * jnp.repeat(draws, extent[dim] // blocks).reshape([-1 if axis == dim else 1 for axis in range(len(extent))])
    return gain


def centred(key, dims, spread, most, pieces=(), held_as=jnp.bfloat16):
    drawn = spread * jax.random.normal(key, dims, jnp.float32)
    if pieces:
        drawn = drawn * levels(key, dims, pieces, -0.22, 0.18)
    return jnp.clip(drawn, -most, most).astype(held_as)


def setup_inputs(seed: int = 0) -> dict:
    key_list = jax.random.split(jax.random.key(seed), 6)
    return {
        "matrix": centred(key_list[0], (NROWS, NCOLS), 1.0, 6.0, ((0, 8), (1, 4)), jnp.float32),
        "leaf_vectors": centred(key_list[1], (TICKS, NROWS, B), M_DEV ** -0.5, 0.09375, ((1, 32),), jnp.float32),
        "leaf_factors": centred(key_list[2], (TICKS, N_ROW * B, B), 0.1, 1.5, ((1, 32),), jnp.float32),
        "tree_vectors": centred(key_list[3], (TICKS, N_ROW * B, B), B ** -0.5, 0.5, ((1, 32),), jnp.float32),
        "tree_factors": centred(key_list[4], (TICKS, N_ROW * B, B), 0.06, 0.875, ((1, 32),), jnp.float32),
    }


def leaf_apply(operands):
    row_block, vectors, factor = operands
    projected = jnp.dot(vectors.T, row_block, precision=lax.Precision.HIGHEST)
    scaled = jnp.dot(jnp.triu(factor).T, projected, precision=lax.Precision.HIGHEST)
    return row_block - jnp.dot(vectors, scaled, precision=lax.Precision.HIGHEST)


def reference(matrix, leaf_vectors, leaf_factors, tree_vectors, tree_factors):
    row_blocks = matrix.reshape(N_ROW, M_DEV, NCOLS)
    hp = lax.Precision.HIGHEST
    for tick_index in range(TICKS):
        vectors = leaf_vectors[tick_index].reshape(N_ROW, M_DEV, B)
        factors = leaf_factors[tick_index].reshape(N_ROW, B, B)
        row_blocks = lax.map(leaf_apply, (row_blocks, vectors, factors))
        top_rows = row_blocks[:, :B, :]
        node_vectors = tree_vectors[tick_index].reshape(N_ROW, B, B)
        node_factors = jnp.triu(tree_factors[tick_index].reshape(N_ROW, B, B))
        for tree_level in range(LEVELS):
            stride = 2 ** tree_level
            upper_ids = jnp.arange(0, N_ROW, 2 * stride)
            lower_ids = upper_ids + stride
            upper_rows = top_rows[upper_ids]
            lower_rows = top_rows[lower_ids]
            vector = node_vectors[lower_ids]
            factor = node_factors[lower_ids]
            summed = upper_rows + jnp.einsum("rab,rac->rbc", vector, lower_rows, precision=hp)
            coupled = jnp.einsum("rab,rac->rbc", factor, summed, precision=hp)
            top_rows = top_rows.at[upper_ids].set(upper_rows - coupled)
            top_rows = top_rows.at[lower_ids].set(lower_rows - jnp.einsum("rab,rbc->rac", vector, coupled, precision=hp))
        row_blocks = row_blocks.at[:, :B, :].set(top_rows)
    return row_blocks.reshape(NROWS, NCOLS)
```

```python
import functools

import jax
import jax.numpy as jnp
from jax import lax
from jax.experimental import pallas as pl
from jax.experimental.pallas import tpu as pltpu
from jax.sharding import PartitionSpec as P

MESH = pl.DeviceIdType.MESH
F32 = jnp.float32
BF16 = jnp.bfloat16
TILE = 512
CHUNKS = 2


def split(x):
    high = x.astype(BF16)
    return high, (x - high.astype(F32)).astype(BF16)


def mm(x, y, contract_x):
    return lax.dot_general(
        x, y, (((contract_x,), (0,)), ((), ())), preferred_element_type=F32
    )


def dot3(x, y, contract_x):
    x_high, x_low = split(x)
    y_high, y_low = split(y)
    return (
        mm(x_high, y_high, contract_x)
        + mm(x_low, y_high, contract_x)
        + mm(x_high, y_low, contract_x)
    )


def upper_triangle(x):
    row = lax.broadcasted_iota(jnp.int32, x.shape, 0)
    col = lax.broadcasted_iota(jnp.int32, x.shape, 1)
    return jnp.where(row <= col, x, 0.0)


def low_bit(mask):
    return mask & -mask


def kernel(
    n_row, n_col,
    a_in, v_in, l_in, y_in, s_in, o_ref,
    a, v, vc, small, lower_s, top, proj, w_cat, w_low, sent, got,
    a_sem, v_own_sem, v_send, v_recv, small_own, small_send, small_recv,
    s_send, s_recv, x_send, x_recv, o_sem, o_top_sem,
):
    panels, shard, width = v_in.shape
    rows, cols = a_in.shape
    part = l_in.shape[1]
    levels = n_row.bit_length() - 1
    tiles = rows // TILE
    chunk = cols // CHUNKS
    r = lax.axis_index("row")
    c = lax.axis_index("col")

    def partner(mask):
        bits = c
        for bit in range(n_col.bit_length() - 1):
            if mask >> bit & 1:
                bits = bits + (1 << bit) - 2 * (1 << bit) * ((bits // (1 << bit)) % 2)
        return bits

    def row_partner(level):
        step = 1 << level
        return r + step - 2 * step * ((r // step) % 2)

    def block_rows(mask):
        return pl.ds(pl.multiple_of(partner(mask) * shard, shard), shard)

    def part_rows(mask):
        return pl.ds(pl.multiple_of(partner(mask) * part, part), part)

    def a_copy(mask):
        return pltpu.make_async_copy(
            a_in.at[block_rows(mask)], a.at[block_rows(mask)], a_sem.at[mask]
        )

    def v_own(k):
        return pltpu.make_async_copy(v_in.at[k], v.at[k, block_rows(0)], v_own_sem.at[k])

    def v_copy(k, mask):
        bit = low_bit(mask)
        held = mask ^ bit
        source = v_in.at[k] if held == 0 else v.at[k, block_rows(held)]
        return pltpu.make_async_remote_copy(
            src_ref=source,
            dst_ref=v.at[k, block_rows(held)],
            send_sem=v_send.at[k, mask],
            recv_sem=v_recv.at[k, mask],
            device_id={"row": r, "col": partner(bit)},
            device_id_type=MESH,
        )

    def small_local(which, source):
        return pltpu.make_async_copy(
            source, small.at[which, :, part_rows(0)], small_own.at[which]
        )

    def small_copy(which, source, mask):
        return pltpu.make_async_remote_copy(
            src_ref=source,
            dst_ref=small.at[which, :, part_rows(0)],
            send_sem=small_send.at[which, mask],
            recv_sem=small_recv.at[which, mask],
            device_id={"row": r, "col": partner(mask)},
            device_id_type=MESH,
        )

    def s_copy(level):
        return pltpu.make_async_remote_copy(
            src_ref=small.at[2],
            dst_ref=lower_s.at[level],
            send_sem=s_send.at[level],
            recv_sem=s_recv.at[level],
            device_id={"row": row_partner(level), "col": c},
            device_id_type=MESH,
        )

    def x_copy(k, level, piece):
        return pltpu.make_async_remote_copy(
            src_ref=sent.at[k, level, piece],
            dst_ref=got.at[k, level, piece],
            send_sem=x_send.at[k, level, piece],
            recv_sem=x_recv.at[k, level, piece],
            device_id={"row": row_partner(level), "col": c},
            device_id_type=MESH,
        )

    def is_lower(level):
        return r % (2 << level) == 1 << level

    def is_upper(level):
        return r % (2 << level) == 0

    def takes_part(level):
        return r % (1 << level) == 0

    masks = range(1, n_col)
    small_in = (l_in, y_in, s_in)

    for mask in range(n_col):
        a_copy(mask).start()
    for k in range(panels):
        v_own(k).start()
    for which in range(3):
        small_local(which, small_in[which]).start()

    barrier = pltpu.get_barrier_semaphore()
    for mask in masks:
        pl.semaphore_signal(
            barrier, inc=1, device_id={"row": r, "col": partner(mask)}, device_id_type=MESH
        )
    for level in range(levels):
        pl.semaphore_signal(
            barrier, inc=1, device_id={"row": row_partner(level), "col": c}, device_id_type=MESH
        )
    pl.semaphore_wait(barrier, n_col - 1 + levels)

    def start_far(k):
        for mask in masks:
            if mask == low_bit(mask) and mask > 1:
                v_copy(k, mask).start()

    def start_near(k):
        if n_col > 1:
            v_copy(k, 1).start()

    start_near(0)
    start_far(0)
    for which in range(3):
        for mask in masks:
            small_copy(which, small_in[which], mask).start()
    for k in range(1, panels):
        start_near(k)

    def project(k, mask):
        base = partner(mask) * shard

        def step(t, carry):
            at = pl.ds(pl.multiple_of(base + t * TILE, TILE), TILE)
            v_high, v_low = split(v[k, at])
            both = jnp.concatenate([v_high, v_low], axis=1)
            vc[at, :] = both
            a_high, a_low = split(a[at, :])
            out = mm(both, a_high, 0)
            proj[...] += out[:width] + out[width:] + mm(v_high, a_low, 0)
            return carry

        lax.fori_loop(0, shard // TILE, step, 0)

    def update(first, last, final):
        def step(t, carry):
            at = pl.ds(pl.multiple_of(t * TILE, TILE), TILE)
            both = vc[at, :]
            a[at, :] = a[at, :] - (
                mm(both, w_cat[...], 1) + mm(both[:, :width], w_low[...], 1)
            )
            if final:
                @pl.when(t > 0)
                def _():
                    pltpu.make_async_copy(a.at[at], o_ref.at[at], o_sem.at[t]).start()
            return carry

        lax.fori_loop(first, last, step, 0)

    def columns(piece):
        return pl.ds(piece * chunk, chunk)

    def send_level(k, level, piece):
        @pl.when(is_lower(level))
        def _():
            sent[k, level, piece] = dot3(small[1, k], top[:, columns(piece)], 0)

        @pl.when(is_upper(level))
        def _():
            sent[k, level, piece] = top[:, columns(piece)]

        @pl.when(takes_part(level))
        def _():
            x_copy(k, level, piece).start()

    def take_level(k, level, piece):
        @pl.when(takes_part(level))
        def _():
            x_copy(k, level, piece).wait_recv()

        @pl.when(is_lower(level))
        def _():
            total = sent[k, level, piece] + got[k, level, piece]
            coupled = dot3(upper_triangle(small[2, k]), total, 0)
            top[:, columns(piece)] -= dot3(small[1, k], coupled, 1)

        @pl.when(is_upper(level))
        def _():
            total = sent[k, level, piece] + got[k, level, piece]
            top[:, columns(piece)] -= dot3(upper_triangle(lower_s[level, k]), total, 0)

    def receive(k, mask):
        v_copy(k, mask).wait_recv()
        bit = 1
        while bit < low_bit(mask):
            v_copy(k, mask | bit).start()
            bit *= 2

    last_direct = n_col // 2
    order = [mask for mask in masks if mask == low_bit(mask)]
    order += [mask for mask in masks if mask != low_bit(mask)]

    proj[...] = jnp.zeros_like(proj)
    a_copy(0).wait()
    v_own(0).wait()
    project(0, 0)

    for k in range(panels):
        for mask in order:
            receive(k, mask)
            if mask == last_direct and k + 1 < panels:
                start_far(k + 1)
            if k == 0:
                a_copy(mask).wait()
            project(k, mask)
        if k == 0:
            top[...] = a[:width, :]
            for which in range(3):
                small_local(which, small_in[which]).wait()
                for mask in masks:
                    small_copy(which, small_in[which], mask).wait_recv()
            for level in range(levels):
                @pl.when(is_lower(level))
                def _():
                    s_copy(level).start()
        else:
            v_high, v_low = split(v[k, pl.ds(0, width)])
            t_high, t_low = split(top[...])
            proj[...] += mm(v_high, t_high, 0) + mm(v_low, t_high, 0) + mm(v_high, t_low, 0)

        w = dot3(upper_triangle(small[0, k]), proj[...], 0)
        w_high, w_small = split(w)
        w_cat[...] = jnp.concatenate([w_high, w_high], axis=0)
        w_low[...] = w_small
        head = vc[pl.ds(0, width), :]
        top[...] -= mm(head, w_cat[...], 1) + mm(head[:, :width], w_low[...], 1)

        for piece in range(CHUNKS):
            send_level(k, 0, piece)
        if k == 0:
            for level in range(levels):
                @pl.when(is_upper(level))
                def _():
                    s_copy(level).wait_recv()
        final = k == panels - 1
        for level in range(levels):
            update(tiles * level // levels, tiles * (level + 1) // levels, final)
            if level == levels - 1:
                if final:
                    rest = pl.ds(width, TILE - width)
                    pltpu.make_async_copy(a.at[rest], o_ref.at[rest], o_sem.at[0]).start()
                else:
                    a[:width, :] = jnp.zeros((width, cols), F32)
                    proj[...] = jnp.zeros_like(proj)
                    v_own(k + 1).wait()
                    project(k + 1, 0)
            for piece in range(CHUNKS):
                take_level(k, level, piece)
                if level + 1 < levels:
                    send_level(k, level + 1, piece)

    head_rows = pl.ds(0, width)
    pltpu.make_async_copy(top, o_ref.at[head_rows], o_top_sem).start()

    for k in range(panels):
        for mask in masks:
            v_copy(k, mask).wait_send()
    for which in range(3):
        for mask in masks:
            small_copy(which, small_in[which], mask).wait_send()
    for level in range(levels):
        @pl.when(is_lower(level))
        def _():
            s_copy(level).wait_send()

        @pl.when(takes_part(level))
        def _():
            for k in range(panels):
                for piece in range(CHUNKS):
                    x_copy(k, level, piece).wait_send()
    rest = pl.ds(width, TILE - width)
    pltpu.make_async_copy(a.at[rest], o_ref.at[rest], o_sem.at[0]).wait()
    for t in range(1, tiles):
        at = pl.ds(t * TILE, TILE)
        pltpu.make_async_copy(a.at[at], o_ref.at[at], o_sem.at[t]).wait()
    pltpu.make_async_copy(top, o_ref.at[head_rows], o_top_sem).wait()


def local(n_row, n_col, matrix, leaf_vectors, leaf_factors, tree_vectors, tree_factors):
    rows, cols = matrix.shape
    panels, shard, width = leaf_vectors.shape
    levels = n_row.bit_length() - 1
    chunk = cols // CHUNKS
    anywhere = pl.BlockSpec(memory_space=pl.ANY)
    dma = pltpu.SemaphoreType.DMA
    return pl.pallas_call(
        functools.partial(kernel, n_row, n_col),
        out_shape=jax.ShapeDtypeStruct((rows, cols), F32),
        in_specs=[anywhere] * 5,
        out_specs=anywhere,
        scratch_shapes=[
            pltpu.VMEM((rows, cols), F32),
            pltpu.VMEM((panels, rows, width), F32),
            pltpu.VMEM((rows, 2 * width), BF16),
            pltpu.VMEM((3, panels, width, width), F32),
            pltpu.VMEM((levels, panels, width, width), F32),
            pltpu.VMEM((width, cols), F32),
            pltpu.VMEM((width, cols), F32),
            pltpu.VMEM((2 * width, cols), BF16),
            pltpu.VMEM((width, cols), BF16),
            pltpu.VMEM((panels, levels, CHUNKS, width, chunk), F32),
            pltpu.VMEM((panels, levels, CHUNKS, width, chunk), F32),
            dma((n_col,)),
            dma((panels,)),
            dma((panels, n_col)),
            dma((panels, n_col)),
            dma((3,)),
            dma((3, n_col)),
            dma((3, n_col)),
            dma((levels,)),
            dma((levels,)),
            dma((panels, levels, CHUNKS)),
            dma((panels, levels, CHUNKS)),
            dma((rows // TILE,)),
            dma(()),
        ],
        compiler_params=pltpu.CompilerParams(
            collective_id=0, has_side_effects=True, vmem_limit_bytes=56 << 20
        ),
    )(matrix, leaf_vectors, leaf_factors, tree_vectors, tree_factors)


def solution(mesh):
    placed = (
        P("row", "col"),
        P(None, ("row", "col"), None),
        P(None, ("row", "col"), None),
        P(None, ("row", "col"), None),
        P(None, ("row", "col"), None),
    )
    return jax.shard_map(
        functools.partial(local, mesh.shape["row"], mesh.shape["col"]),
        mesh=mesh, in_specs=placed, out_specs=P("row", "col"), check_vma=False,
    )
```

```python
import functools

import jax
import jax.numpy as jnp
from jax import lax
from jax.experimental import pallas as pl
from jax.experimental.pallas import tpu as pltpu
from jax.sharding import PartitionSpec as P

MESH = pl.DeviceIdType.MESH
F32 = jnp.float32
BF16 = jnp.bfloat16
TILE = 512
CHUNKS = 2


def split(x):
    high = x.astype(BF16)
    return high, (x - high.astype(F32)).astype(BF16)


def mm(x, y, contract_x):
    return lax.dot_general(
        x, y, (((contract_x,), (0,)), ((), ())), preferred_element_type=F32
    )


def dot3(x, y, contract_x):
    x_high, x_low = split(x)
    y_high, y_low = split(y)
    return (
        mm(x_high, y_high, contract_x)
        + mm(x_low, y_high, contract_x)
        + mm(x_high, y_low, contract_x)
    )


def upper_triangle(x):
    row = lax.broadcasted_iota(jnp.int32, x.shape, 0)
    col = lax.broadcasted_iota(jnp.int32, x.shape, 1)
    return jnp.where(row <= col, x, 0.0)


def low_bit(mask):
    return mask & -mask


def kernel(
    n_row, n_col,
    a_in, v_in, l_in, y_in, s_in, o_ref,
    a, v, vc, small, lower_s, top, proj, w_cat, w_low, sent, got,
    a_sem, v_own_sem, v_send, v_recv, small_own, small_send, small_recv,
    s_send, s_recv, x_send, x_recv, o_sem, o_top_sem,
):
    panels, shard, width = v_in.shape
    rows, cols = a_in.shape
    part = l_in.shape[1]
    levels = n_row.bit_length() - 1
    tiles = rows // TILE
    chunk = cols // CHUNKS
    r = lax.axis_index("row")
    c = lax.axis_index("col")

    def partner(mask):
        bits = c
        for bit in range(n_col.bit_length() - 1):
            if mask >> bit & 1:
                bits = bits + (1 << bit) - 2 * (1 << bit) * ((bits // (1 << bit)) % 2)
        return bits

    def row_partner(level):
        step = 1 << level
        return r + step - 2 * step * ((r // step) % 2)

    def block_rows(mask):
        return pl.ds(pl.multiple_of(partner(mask) * shard, shard), shard)

    def part_rows(mask):
        return pl.ds(pl.multiple_of(partner(mask) * part, part), part)

    def a_copy(mask):
        return pltpu.make_async_copy(
            a_in.at[block_rows(mask)], a.at[block_rows(mask)], a_sem.at[mask]
        )

    def v_own(k):
        return pltpu.make_async_copy(v_in.at[k], v.at[k, block_rows(0)], v_own_sem.at[k])

    def v_copy(k, mask):
        bit = low_bit(mask)
        held = mask ^ bit
        source = v_in.at[k] if held == 0 else v.at[k, block_rows(held)]
        return pltpu.make_async_remote_copy(
            src_ref=source,
            dst_ref=v.at[k, block_rows(held)],
            send_sem=v_send.at[k, mask],
            recv_sem=v_recv.at[k, mask],
            device_id={"row": r, "col": partner(bit)},
            device_id_type=MESH,
        )

    def small_local(which, source):
        return pltpu.make_async_copy(
            source, small.at[which, :, part_rows(0)], small_own.at[which]
        )

    def small_copy(which, mask):
        bit = low_bit(mask)
        held = mask ^ bit
        there = small.at[which, :, part_rows(held)]
        return pltpu.make_async_remote_copy(
            src_ref=small_in[which] if held == 0 else there,
            dst_ref=there,
            send_sem=small_send.at[which, mask],
            recv_sem=small_recv.at[which, mask],
            device_id={"row": r, "col": partner(bit)},
            device_id_type=MESH,
        )

    def s_copy(level):
        return pltpu.make_async_remote_copy(
            src_ref=small.at[2],
            dst_ref=lower_s.at[level],
            send_sem=s_send.at[level],
            recv_sem=s_recv.at[level],
            device_id={"row": row_partner(level), "col": c},
            device_id_type=MESH,
        )

    def x_copy(k, level, piece):
        return pltpu.make_async_remote_copy(
            src_ref=sent.at[k, level, piece],
            dst_ref=got.at[k, level, piece],
            send_sem=x_send.at[k, level, piece],
            recv_sem=x_recv.at[k, level, piece],
            device_id={"row": row_partner(level), "col": c},
            device_id_type=MESH,
        )

    def is_lower(level):
        return r % (2 << level) == 1 << level

    def is_upper(level):
        return r % (2 << level) == 0

    def takes_part(level):
        return r % (1 << level) == 0

    masks = range(1, n_col)
    direct = [mask for mask in masks if mask == low_bit(mask)]
    relayed = [mask for mask in masks if mask != low_bit(mask)]
    small_in = (l_in, y_in, s_in)

    for mask in range(n_col):
        a_copy(mask).start()
    for k in range(panels):
        v_own(k).start()
    for which in range(3):
        small_local(which, small_in[which]).start()

    barrier = pltpu.get_barrier_semaphore()
    for mask in masks:
        pl.semaphore_signal(
            barrier, inc=1, device_id={"row": r, "col": partner(mask)}, device_id_type=MESH
        )
    for level in range(levels):
        pl.semaphore_signal(
            barrier, inc=1, device_id={"row": row_partner(level), "col": c}, device_id_type=MESH
        )
    pl.semaphore_wait(barrier, n_col - 1 + levels)

    def start_far(k):
        for mask in masks:
            if mask == low_bit(mask) and mask > 1:
                v_copy(k, mask).start()

    def start_near(k):
        if n_col > 1:
            v_copy(k, 1).start()

    start_near(0)
    start_far(0)
    for which in range(3):
        for mask in direct:
            small_copy(which, mask).start()
    for k in range(1, panels):
        start_near(k)

    def project(k, mask):
        base = partner(mask) * shard

        def step(t, carry):
            at = pl.ds(pl.multiple_of(base + t * TILE, TILE), TILE)
            v_high, v_low = split(v[k, at])
            both = jnp.concatenate([v_high, v_low], axis=1)
            vc[at, :] = both
            a_high, a_low = split(a[at, :])
            out = mm(both, a_high, 0)
            proj[...] += out[:width] + out[width:] + mm(v_high, a_low, 0)
            return carry

        lax.fori_loop(0, shard // TILE, step, 0)

    def update(first, last, final):
        def step(t, carry):
            at = pl.ds(pl.multiple_of(t * TILE, TILE), TILE)
            both = vc[at, :]
            a[at, :] = a[at, :] - (
                mm(both, w_cat[...], 1) + mm(both[:, :width], w_low[...], 1)
            )
            if final:
                @pl.when(t > 0)
                def _():
                    pltpu.make_async_copy(a.at[at], o_ref.at[at], o_sem.at[t]).start()
            return carry

        lax.fori_loop(first, last, step, 0)

    def columns(piece):
        return pl.ds(piece * chunk, chunk)

    def send_level(k, level, piece):
        @pl.when(is_lower(level))
        def _():
            sent[k, level, piece] = dot3(small[1, k], top[:, columns(piece)], 0)

        @pl.when(is_upper(level))
        def _():
            sent[k, level, piece] = top[:, columns(piece)]

        @pl.when(takes_part(level))
        def _():
            x_copy(k, level, piece).start()

    def take_level(k, level, piece):
        @pl.when(takes_part(level))
        def _():
            x_copy(k, level, piece).wait_recv()

        @pl.when(is_lower(level))
        def _():
            total = sent[k, level, piece] + got[k, level, piece]
            coupled = dot3(upper_triangle(small[2, k]), total, 0)
            top[:, columns(piece)] -= dot3(small[1, k], coupled, 1)

        @pl.when(is_upper(level))
        def _():
            total = sent[k, level, piece] + got[k, level, piece]
            top[:, columns(piece)] -= dot3(upper_triangle(lower_s[level, k]), total, 0)

    def relay_small(mask):
        for which in range(3):
            small_copy(which, mask).wait_recv()
            bit = 1
            while bit < low_bit(mask):
                small_copy(which, mask | bit).start()
                bit *= 2

    def receive(k, mask):
        v_copy(k, mask).wait_recv()
        bit = 1
        while bit < low_bit(mask):
            v_copy(k, mask | bit).start()
            bit *= 2

    last_direct = n_col // 2
    order = direct + relayed

    proj[...] = jnp.zeros_like(proj)
    a_copy(0).wait()
    v_own(0).wait()
    project(0, 0)

    for k in range(panels):
        for mask in order:
            receive(k, mask)
            if mask == last_direct and k + 1 < panels:
                start_far(k + 1)
            if k == 0:
                a_copy(mask).wait()
                relay_small(mask)
            project(k, mask)
        if k == 0:
            top[...] = a[:width, :]
            for which in range(3):
                small_local(which, small_in[which]).wait()
            for level in range(levels):
                @pl.when(is_lower(level))
                def _():
                    s_copy(level).start()
        else:
            v_high, v_low = split(v[k, pl.ds(0, width)])
            t_high, t_low = split(top[...])
            proj[...] += mm(v_high, t_high, 0) + mm(v_low, t_high, 0) + mm(v_high, t_low, 0)

        w = dot3(upper_triangle(small[0, k]), proj[...], 0)
        w_high, w_small = split(w)
        w_cat[...] = jnp.concatenate([w_high, w_high], axis=0)
        w_low[...] = w_small
        head = vc[pl.ds(0, width), :]
        top[...] -= mm(head, w_cat[...], 1) + mm(head[:, :width], w_low[...], 1)

        for piece in range(CHUNKS):
            send_level(k, 0, piece)
        if k == 0:
            for level in range(levels):
                @pl.when(is_upper(level))
                def _():
                    s_copy(level).wait_recv()
        final = k == panels - 1
        for level in range(levels):
            update(tiles * level // levels, tiles * (level + 1) // levels, final)
            if level == levels - 1:
                if final:
                    rest = pl.ds(width, TILE - width)
                    pltpu.make_async_copy(a.at[rest], o_ref.at[rest], o_sem.at[0]).start()
                else:
                    a[:width, :] = jnp.zeros((width, cols), F32)
                    proj[...] = jnp.zeros_like(proj)
                    v_own(k + 1).wait()
                    project(k + 1, 0)
            for piece in range(CHUNKS):
                take_level(k, level, piece)
                if level + 1 < levels:
                    send_level(k, level + 1, piece)

    head_rows = pl.ds(0, width)
    pltpu.make_async_copy(top, o_ref.at[head_rows], o_top_sem).start()

    for k in range(panels):
        for mask in masks:
            v_copy(k, mask).wait_send()
    for which in range(3):
        for mask in masks:
            small_copy(which, mask).wait_send()
    for level in range(levels):
        @pl.when(is_lower(level))
        def _():
            s_copy(level).wait_send()

        @pl.when(takes_part(level))
        def _():
            for k in range(panels):
                for piece in range(CHUNKS):
                    x_copy(k, level, piece).wait_send()
    rest = pl.ds(width, TILE - width)
    pltpu.make_async_copy(a.at[rest], o_ref.at[rest], o_sem.at[0]).wait()
    for t in range(1, tiles):
        at = pl.ds(t * TILE, TILE)
        pltpu.make_async_copy(a.at[at], o_ref.at[at], o_sem.at[t]).wait()
    pltpu.make_async_copy(top, o_ref.at[head_rows], o_top_sem).wait()


def local(n_row, n_col, matrix, leaf_vectors, leaf_factors, tree_vectors, tree_factors):
    rows, cols = matrix.shape
    panels, shard, width = leaf_vectors.shape
    levels = n_row.bit_length() - 1
    chunk = cols // CHUNKS
    anywhere = pl.BlockSpec(memory_space=pl.ANY)
    dma = pltpu.SemaphoreType.DMA
    return pl.pallas_call(
        functools.partial(kernel, n_row, n_col),
        out_shape=jax.ShapeDtypeStruct((rows, cols), F32),
        in_specs=[anywhere] * 5,
        out_specs=anywhere,
        scratch_shapes=[
            pltpu.VMEM((rows, cols), F32),
            pltpu.VMEM((panels, rows, width), F32),
            pltpu.VMEM((rows, 2 * width), BF16),
            pltpu.VMEM((3, panels, width, width), F32),
            pltpu.VMEM((levels, panels, width, width), F32),
            pltpu.VMEM((width, cols), F32),
            pltpu.VMEM((width, cols), F32),
            pltpu.VMEM((2 * width, cols), BF16),
            pltpu.VMEM((width, cols), BF16),
            pltpu.VMEM((panels, levels, CHUNKS, width, chunk), F32),
            pltpu.VMEM((panels, levels, CHUNKS, width, chunk), F32),
            dma((n_col,)),
            dma((panels,)),
            dma((panels, n_col)),
            dma((panels, n_col)),
            dma((3,)),
            dma((3, n_col)),
            dma((3, n_col)),
            dma((levels,)),
            dma((levels,)),
            dma((panels, levels, CHUNKS)),
            dma((panels, levels, CHUNKS)),
            dma((rows // TILE,)),
            dma(()),
        ],
        compiler_params=pltpu.CompilerParams(
            collective_id=0, has_side_effects=True, vmem_limit_bytes=56 << 20
        ),
    )(matrix, leaf_vectors, leaf_factors, tree_vectors, tree_factors)


def solution(mesh):
    placed = (
        P("row", "col"),
        P(None, ("row", "col"), None),
        P(None, ("row", "col"), None),
        P(None, ("row", "col"), None),
        P(None, ("row", "col"), None),
    )
    return jax.shard_map(
        functools.partial(local, mesh.shape["row"], mesh.shape["col"]),
        mesh=mesh, in_specs=placed, out_specs=P("row", "col"), check_vma=False,
    )
```
